32 devices in a mesh: shard: 8 (over y, x, core), seq: 4 (over z).
Axes of the slice: x: 2, y: 2, z: 4, core: 2. Of those that a mesh axis runs over, the one named last changes fastest.
Arguments:
- tokens: bfloat16 [16, 1024, 1152], P('shard', 'seq'), may hold values from -6 to 6
- cond: bfloat16 [16, 1152], P('shard'), may hold values from -6 to 6
- d_out: bfloat16 [16, 1024, 1152], P('shard', 'seq'), may hold values from -6 to 6
- w_qkv: bfloat16 [1152, 3456], P(('shard', 'seq')), may hold values from -0.1875 to 0.1875
- bias_qv: bfloat16 [2304], P(('shard', 'seq')), may hold values from -1.796875 to 1.796875
- w_proj: bfloat16 [1152, 1152], P(('shard', 'seq')), may hold values from -0.75 to 0.75
- b_proj: bfloat16 [1152], P(('shard', 'seq')), may hold values from -1.796875 to 1.796875
- w_fc1: bfloat16 [1152, 4608], P(('shard', 'seq')), may hold values from -0.1875 to 0.1875
- b_fc1: bfloat16 [4608], P(('shard', 'seq')), may hold values from -1.796875 to 1.796875
- w_fc2: bfloat16 [4608, 1152], P(('shard', 'seq')), may hold values from -0.09375 to 0.09375
- b_fc2: bfloat16 [1152], P(('shard', 'seq')), may hold values from -1.796875 to 1.796875
- w_ada: bfloat16 [1152, 6912], P(('shard', 'seq')), may hold values from -0.1875 to 0.1875
- b_ada: bfloat16 [6912], P(('shard', 'seq')), may hold values from -3 to 3
Outputs:
- output: bfloat16 [16, 1024, 1152], P('shard', 'seq')
- grad_tokens: float32 [16, 1024, 1152], P('shard', 'seq')
- grad_cond: float32 [16, 1152], P('shard')
- grad_w_qkv: float32 [1152, 3456], P(('shard', 'seq'))
- grad_bias_qv: float32 [2304], P(('shard', 'seq'))
- grad_w_proj: float32 [1152, 1152], P(('shard', 'seq'))
- grad_b_proj: float32 [1152], P(('shard', 'seq'))
- grad_w_fc1: float32 [1152, 4608], P(('shard', 'seq'))
- grad_b_fc1: float32 [4608], P(('shard', 'seq'))
- grad_w_fc2: float32 [4608, 1152], P(('shard', 'seq'))
- grad_b_fc2: float32 [1152], P(('shard', 'seq'))
- grad_w_ada: float32 [1152, 6912], P(('shard', 'seq'))
- grad_b_ada: float32 [6912], P(('shard', 'seq'))
The draws below stay inside these ranges and needn't reach their ends.
All inputs are finite; a program needn't handle non-finite values.
Results may differ from the reference program's by a relative error of at most 0.018.
Values may be sent and summed in bfloat16 or wider, within the bound.
No kernel may reach another device: no remote copies, remote signals or barrier semaphores. Data moves between devices by JAX's collectives and lax.ppermute only.
A program may use at most 320 MiB of HBM per device.

```python
import math
import jax
import jax.numpy as jnp
from jax import lax

D = 1152
HEADS = 16
HEAD = 72
FF = 4608
LENGTH = 1024
LATENTS = 16


def shard_levels(stream_key, dims, cuts, least, high):
    factor_of, own = 1.0, jax.random.fold_in(stream_key, 6)
    for dim, parts in cuts:
        steps = jnp.exp(jax.random.uniform(jax.random.fold_in(own, dim), (parts,), jnp.float32, least / len(cuts), high / len(cuts)))
        factor_of = factor_of * jnp.repeat(steps, dims[dim] // parts).reshape([-1 if axis == dim else 1 for axis in range(len(dims))])
    return factor_of


def bell_draw(key, extent, scale, reach, pieces=(), kind=jnp.bfloat16):
    entries = jax.random.normal(key, extent, jnp.float32) * scale
    if len(pieces) > 0:
        entries = shard_levels(key, extent, pieces, -0.22, 0.18) * entries
    return jnp.clip(entries, min=-reach, max=reach).astype(kind)


def setup_inputs(seed: int = 0) -> dict:
    key_of = jax.random.split(jax.random.key(seed), 14)
    tokens = bell_draw(key_of[0], (LATENTS, LENGTH, D), 1.0, 6.0, ((0, 8), (1, 4)))
    cond = bell_draw(key_of[1], (LATENTS, D), 1.0, 6.0, ((0, 8),))
    d_out = bell_draw(key_of[2], (LATENTS, LENGTH, D), 1.0, 6.0, ((0, 8), (1, 4)))
    w_qkv = bell_draw(key_of[3], (D, 3 * D), D ** -0.5, 0.1875, ((0, 32),))
    bias_qv = bell_draw(key_of[4], (2 * D,), 0.3, 1.796875, ((0, 32),))
    w_proj = bell_draw(key_of[5], (D, D), (D // 16) ** -0.5, 0.75, ((0, 32),))
    b_proj = bell_draw(key_of[6], (D,), 0.3, 1.796875, ((0, 32),))
    w_fc1 = bell_draw(key_of[7], (D, FF), D ** -0.5, 0.1875, ((0, 32),))
    b_fc1 = bell_draw(key_of[8], (FF,), 0.3, 1.796875, ((0, 32),))
    w_fc2 = bell_draw(key_of[9], (FF, D), FF ** -0.5, 0.09375, ((0, 32),))
    b_fc2 = bell_draw(key_of[10], (D,), 0.3, 1.796875, ((0, 32),))
    w_ada = bell_draw(key_of[11], (D, 6 * D), D ** -0.5, 0.1875, ((0, 32),))
    b_ada = bell_draw(key_of[12], (6 * D,), 0.5, 3.0, ((0, 32),))
    return {"tokens": tokens, "cond": cond, "d_out": d_out, "w_qkv": w_qkv, "bias_qv": bias_qv, "w_proj": w_proj, "b_proj": b_proj, "w_fc1": w_fc1, "b_fc1": b_fc1, "w_fc2": w_fc2, "b_fc2": b_fc2, "w_ada": w_ada, "b_ada": b_ada}


HIGHEST = lax.Precision.HIGHEST
NORM_EPS = 1e-06
GELU_SCALE = 0.7978845608028654
CUBIC = 0.044715

@jax.custom_vjp
def low(v):
    return lax.optimization_barrier(v.astype(jnp.bfloat16)).astype(jnp.float32)

@jax.custom_vjp
def low_back(v):
    return v

def low_keep(v):
    return (low(v), None)

def low_pass(kept, grad):
    return (grad,)

def back_keep(v):
    return (v, None)

def back_low(kept, grad):
    return (low(grad),)
low.defvjp(low_keep, low_pass)
low_back.defvjp(back_keep, back_low)

def product(left_mat, right_mat):
    return jnp.dot(left_mat, right_mat, precision=HIGHEST, preferred_element_type=jnp.float32)

def gelu_tanh(residual_rows):
    return 0.5 * residual_rows * (1.0 + jnp.tanh(GELU_SCALE * (residual_rows + CUBIC * residual_rows * residual_rows * residual_rows)))

def modulated_norm(residual_rows, shift_vec, scale_vec):
    row_mean = lax.optimization_barrier(jnp.mean(residual_rows, axis=-1, keepdims=True))
    centred = residual_rows - row_mean
    row_var = lax.optimization_barrier(jnp.mean(centred * centred, axis=-1, keepdims=True))
    normed = centred * lax.rsqrt(row_var + NORM_EPS)
    return normed * (1.0 + scale_vec) + shift_vec

def layer(residual_rows, cond_vec, w_qkv, bias_qv, w_proj, b_proj, w_fc1, b_fc1, w_fc2, b_fc2, w_ada, b_ada):
    silu_low = low(jax.nn.silu(cond_vec))
    modulation_table = low_back(product(silu_low[None, :], w_ada)[0] + b_ada)
    selfattend_shift, selfattend_scale, selfattend_gate, feedforward_shift, feedforward_scale, feedforward_gate = jnp.split(modulation_table, 6)
    attention_input_rows = low(modulated_norm(residual_rows, selfattend_shift, selfattend_scale))
    bias_full = jnp.concatenate([bias_qv[:D], jnp.zeros((D,), bias_qv.dtype), bias_qv[D:]])
    qkv = low(low_back(product(attention_input_rows, w_qkv) + bias_full))
    queries = qkv[:, :D].reshape(LENGTH, HEADS, HEAD)
    key_rows = qkv[:, D:2 * D].reshape(LENGTH, HEADS, HEAD)
    value_rows = qkv[:, 2 * D:].reshape(LENGTH, HEADS, HEAD)
    score_scale = 1.0 / math.sqrt(HEAD)
    scores = low_back(jnp.einsum('qhd,khd->hqk', queries, key_rows, precision=HIGHEST) * score_scale)
    row_max = lax.optimization_barrier(jnp.max(scores, axis=-1, keepdims=True))
    expd = jnp.exp(scores - row_max)
    probs = low(expd / lax.optimization_barrier(jnp.sum(expd, axis=-1, keepdims=True)))
    mixed = jnp.einsum('hqk,khd->qhd', probs, value_rows, precision=HIGHEST).reshape(LENGTH, D)
    mixed = low(low_back(mixed))
    attention_result = low_back(product(mixed, w_proj) + b_proj)
    middle_residual = residual_rows + selfattend_gate * attention_result
    mlp_input = low(modulated_norm(middle_residual, feedforward_shift, feedforward_scale))
    up_proj = low_back(product(mlp_input, w_fc1) + b_fc1)
    activated = low(gelu_tanh(up_proj))
    ff_out = low_back(product(activated, w_fc2) + b_fc2)
    return middle_residual + feedforward_gate * ff_out

def reference(tokens, cond, d_out, w_qkv, bias_qv, w_proj, b_proj, w_fc1, b_fc1, w_fc2, b_fc2, w_ada, b_ada):
    params = tuple((weight.astype(jnp.float32) for weight in (w_qkv, bias_qv, w_proj, b_proj, w_fc1, b_fc1, w_fc2, b_fc2, w_ada, b_ada)))

    def per_latent(running, latent_item):
        residual_rows, cond_vec, cotangent = latent_item
        result, pull_back = jax.vjp(layer, residual_rows.astype(jnp.float32), cond_vec.astype(jnp.float32), *params)
        gradients = pull_back(cotangent.astype(jnp.float32))
        running = tuple((left_term + right_term for left_term, right_term in zip(running, gradients[2:])))
        return (running, (result.astype(jnp.bfloat16), gradients[0], gradients[1]))
    zero_grads = tuple((jnp.zeros(weight.shape, jnp.float32) for weight in params))
    totals, (output, grad_tokens, grad_cond) = lax.scan(per_latent, zero_grads, (tokens, cond, d_out))
    return (output, grad_tokens, grad_cond, totals[0], totals[1], totals[2], totals[3], totals[4], totals[5], totals[6], totals[7], totals[8], totals[9])
```

```python
import math

import jax
import jax.numpy as jnp
from jax import lax
from jax.experimental import pallas as pl
from jax.experimental.pallas import tpu as pltpu
from jax.sharding import PartitionSpec as P

HEAD = 72
NORM_EPS = 1e-06
GELU_SCALE = 0.7978845608028654
CUBIC = 0.044715
ALL = ("shard", "seq")
BF = jnp.bfloat16
F32 = jnp.float32
HI = lax.Precision.HIGHEST


def dotf(a, b, ca, cb):
    return lax.dot_general(a, b, (((ca,), (cb,)), ((), ())), preferred_element_type=F32)


class Net:
    def __init__(self, shards, seqs):
        self.S, self.Q = shards, seqs
        bits = shards.bit_length() - 1
        masks = [1 << (j + 1) for j in range(bits - 1)]
        swapped = list(masks)
        for j in range(0, len(masks) - 1, 2):
            swapped[j], swapped[j + 1] = masks[j + 1], masks[j]
        self.masks = (masks, swapped)
        self.P = len(masks)

    def flat(self, s, z):
        return s * self.Q + z

    def perm(self, fn):
        pairs = []
        for s in range(self.S):
            for z in range(self.Q):
                t = fn(s, z)
                if t is not None:
                    pairs.append((self.flat(s, z), self.flat(*t)))
        return pairs

    def send(self, x, fn):
        return lax.ppermute(x, ALL, self.perm(fn))

    def phase(self, x, j):
        return self.send(x, lambda s, z: (s ^ self.masks[s & 1][j], z))

    def core(self, x):
        return self.send(x, lambda s, z: (s ^ 1, z))

    def up(self, x, low=0, high=None):
        high = self.Q - 1 if high is None else high
        return self.send(x, lambda s, z: (s, z + 1) if low <= z < high else None)

    def down(self, x, low=0, high=None):
        high = self.Q - 1 if high is None else high
        return self.send(x, lambda s, z: (s, z - 1) if low < z <= high else None)

    def rotate(self, x, r):
        return self.send(x, lambda s, z: (s, (z - r) % self.Q))

    def line_gather(self, x):
        Q = self.Q
        ups, downs = [x], [x]
        for k in range(1, Q):
            ups.append(self.up(ups[-1], low=k - 1))
            downs.append(self.down(downs[-1], high=Q - k))
        return [x] + [ups[Q - r] + downs[r] for r in range(1, Q)]

    def line_reduce(self, pieces):
        Q = self.Q
        up = down = None
        for k in range(1, Q):
            a, b = pieces[Q - k].astype(F32), pieces[k].astype(F32)
            if up is not None:
                a, b = a + up.astype(F32), b + down.astype(F32)
            up = self.up(a.astype(BF), high=k)
            down = self.down(b.astype(BF), low=Q - 1 - k)
        return pieces[0].astype(F32) + up.astype(F32) + down.astype(F32)

    def gather_blocks(self, block):
        blocks = [block]
        for j in range(self.P):
            blocks = blocks + [self.phase(b, j) for b in blocks]
        return blocks + [self.core(b) for b in blocks]

    def gather(self, x):
        zb = lax.optimization_barrier(jnp.concatenate(self.line_gather(x), axis=0))
        return self.gather_blocks(zb)

    def reduce(self, other, own, axis_rows):
        cur = own.astype(F32) + self.core(other.astype(BF)).astype(F32)
        for j in reversed(range(self.P)):
            half = cur.shape[0] // 2
            got = self.phase(cur[half:].astype(BF), j)
            cur = cur[:half] + got.astype(F32)
        return self.line_reduce([cur[r * axis_rows : (r + 1) * axis_rows] for r in range(self.Q)])

    def shard_of(self, s, block):
        dc = block >> self.P
        c = (s & 1) ^ dc
        out = s ^ dc
        for j in range(self.P):
            m = jnp.where(c == 0, self.masks[0][j], self.masks[1][j])
            out = out ^ jnp.where((block >> j) & 1 == 1, m, 0)
        return out

    def column_of(self, s, block):
        out = s
        for j in range(self.P):
            m = jnp.where((s & 1) == 0, self.masks[0][j], self.masks[1][j])
            out = out ^ jnp.where((block >> j) & 1 == 1, m, 0)
        return out >> 1

    def small_gather(self, x):
        zb = jnp.concatenate([x] + [self.rotate(x, r) for r in range(1, self.Q)], axis=0)
        cur = zb
        for j in range(self.P):
            cur = jnp.concatenate([cur, self.phase(cur, j)], axis=0)
        return cur

    def small_rotate_sum(self, pieces):
        out = pieces[0]
        for r in range(1, self.Q):
            out = out + self.send(pieces[r], lambda s, z, r=r: (s, (z + r) % self.Q))
        return out


def attn_fwd_kernel(q_ref, k0_ref, v0_ref, k1_ref, v1_ref, o_ref, lse_ref):
    scale = math.log2(math.e) / math.sqrt(HEAD)
    q = q_ref[...]
    s0 = dotf(k0_ref[...], q, 0, 0) * scale
    s1 = dotf(k1_ref[...], q, 0, 0) * scale
    top = jnp.maximum(
        jnp.max(s0, axis=0, keepdims=True), jnp.max(s1, axis=0, keepdims=True)
    )
    p0 = jnp.exp2(s0 - top)
    p1 = jnp.exp2(s1 - top)
    total = jnp.sum(p0, axis=0, keepdims=True) + jnp.sum(p1, axis=0, keepdims=True)
    acc = dotf(v0_ref[...], p0.astype(BF), 1, 0) + dotf(v1_ref[...], p1.astype(BF), 1, 0)
    o_ref[...] = (acc * (1.0 / total)).astype(BF)
    lse_ref[...] = (top + jnp.log2(total))[None]


def attn_bwd_kernel(
    q_ref, k0_ref, v0_ref, k1_ref, v1_ref, do_ref, lse_ref, dq_ref, dk0_ref, dv0_ref, dk1_ref, dv1_ref
):
    unit = 1.0 / math.sqrt(HEAD)
    scale = math.log2(math.e) * unit
    q, do, lse = q_ref[...], do_ref[...], lse_ref[0]
    k0, k1 = k0_ref[...], k1_ref[...]
    p0 = jnp.exp2(dotf(k0, q, 0, 0) * scale - lse)
    p1 = jnp.exp2(dotf(k1, q, 0, 0) * scale - lse)
    dp0 = dotf(v0_ref[...], do, 0, 0)
    dp1 = dotf(v1_ref[...], do, 0, 0)
    delta = jnp.sum(p0 * dp0, axis=0, keepdims=True) + jnp.sum(p1 * dp1, axis=0, keepdims=True)
    ds0 = (p0 * (dp0 - delta)).astype(BF)
    ds1 = (p1 * (dp1 - delta)).astype(BF)
    dq_ref[...] = ((dotf(k0, ds0, 1, 0) + dotf(k1, ds1, 1, 0)) * unit).astype(BF)
    dk0_ref[...] = dotf(q, ds0, 1, 1) * unit
    dk1_ref[...] = (dotf(q, ds1, 1, 1) * unit).astype(BF)
    dv0_ref[...] = dotf(do, p0.astype(BF), 1, 1)
    dv1_ref[...] = dotf(do, p1.astype(BF), 1, 1).astype(BF)


def attention(qkv_t, other_t):
    heads = qkv_t.shape[0] // (3 * HEAD)
    n = qkv_t.shape[1]
    spec = lambda off: pl.BlockSpec((HEAD, n), lambda h, off=off: (h + off, 0))
    flops = heads * n * 2 * n * HEAD * 4
    return pl.pallas_call(
        attn_fwd_kernel,
        grid=(heads,),
        in_specs=[spec(0), spec(heads), spec(2 * heads), spec(0), spec(heads)],
        out_specs=[spec(0), pl.BlockSpec((1, 1, n), lambda h: (h, 0, 0))],
        out_shape=[
            jax.ShapeDtypeStruct((heads * HEAD, n), BF),
            jax.ShapeDtypeStruct((heads, 1, n), F32),
        ],
        cost_estimate=pl.CostEstimate(
            flops=flops, transcendentals=heads * n * 2 * n, bytes_accessed=6 * heads * HEAD * n * 2
        ),
        compiler_params=pltpu.CompilerParams(dimension_semantics=("arbitrary",)),
        name="attn_fwd",
    )(qkv_t, qkv_t, qkv_t, other_t, other_t)


def attention_back(qkv_t, other_t, do_t, lse):
    heads = qkv_t.shape[0] // (3 * HEAD)
    n = qkv_t.shape[1]
    spec = lambda off: pl.BlockSpec((HEAD, n), lambda h, off=off: (h + off, 0))
    flops = heads * n * 2 * n * HEAD * 10
    small = jax.ShapeDtypeStruct((heads * HEAD, n), BF)
    wide = jax.ShapeDtypeStruct((heads * HEAD, n), F32)
    return pl.pallas_call(
        attn_bwd_kernel,
        grid=(heads,),
        in_specs=[
            spec(0), spec(heads), spec(2 * heads), spec(0), spec(heads), spec(0),
            pl.BlockSpec((1, 1, n), lambda h: (h, 0, 0)),
        ],
        out_specs=[spec(0)] * 5,
        out_shape=[small, wide, wide, small, small],
        cost_estimate=pl.CostEstimate(
            flops=flops, transcendentals=heads * n * 2 * n, bytes_accessed=14 * heads * HEAD * n * 2
        ),
        compiler_params=pltpu.CompilerParams(dimension_semantics=("arbitrary",)),
        name="attn_bwd",
    )(qkv_t, qkv_t, qkv_t, other_t, other_t, do_t, lse)


def norm_stats(v):
    mean = jnp.mean(v, axis=-1, keepdims=True)
    centred = v - mean
    var = jnp.mean(centred * centred, axis=-1, keepdims=True)
    inv = lax.rsqrt(var + NORM_EPS)
    return centred * inv, inv


def norm_back(grad, normed, inv, scale):
    d_shift = jnp.sum(grad, axis=0)
    d_scale = jnp.sum(grad * normed, axis=0)
    e = grad * (1.0 + scale)
    m1 = jnp.mean(e, axis=-1, keepdims=True)
    m2 = jnp.mean(e * normed, axis=-1, keepdims=True)
    return (e - m1 - normed * m2) * inv, d_shift, d_scale


def gelu_tanh(u):
    return 0.5 * u * (1.0 + jnp.tanh(GELU_SCALE * (u + CUBIC * u * u * u)))


def gelu_slope(u):
    t = jnp.tanh(GELU_SCALE * (u + CUBIC * u * u * u))
    return 0.5 * (1.0 + t) + 0.5 * u * (1.0 - t * t) * GELU_SCALE * (1.0 + 3.0 * CUBIC * u * u)


def make_body(S, Q):
    net = Net(S, Q)

    def body(
        tokens, cond, d_out, w_qkv, bias_qv, w_proj, b_proj, w_fc1, b_fc1, w_fc2, b_fc2, w_ada, b_ada
    ):
        s, z = lax.axis_index("shard"), lax.axis_index("seq")
        me = s * Q + z
        per, rows, width = tokens.shape
        piece = w_qkv.shape[0]
        fpiece = w_fc2.shape[0]
        hidden = w_fc1.shape[1]
        mods = w_ada.shape[1]
        latents = per * S
        assert per == 2 and Q == 2 * per

        def spread(x, j):
            block = jnp.where(((z + j) & 1) == 0, x[0], x[1])
            return net.send(
                block,
                lambda a, b: (a - (a & 1) + b // 2, 2 * (a & 1) + (b + j) % 2),
            )

        def back(x, j):
            inverse = {}
            for a in range(S):
                for b in range(Q):
                    inverse[(a - (a & 1) + b // 2, 2 * (a & 1) + (b + j) % 2)] = (a, b)
            return net.send(x, lambda a, b: inverse[(a, b)])

        def collect(x):
            return jnp.concatenate([spread(x, 0), spread(x, 1)], axis=0)

        def give_back(x):
            b0, b1 = back(x[:rows], 0), back(x[rows:], 1)
            even = (z & 1) == 0
            return jnp.stack([jnp.where(even, b0, b1), jnp.where(even, b1, b0)], axis=0)

        ids = jnp.arange(S * Q)
        src_piece = net.shard_of(s, ids // Q) * Q + (z + ids % Q) % Q
        src_rows = jnp.repeat(src_piece * piece, piece) + jnp.tile(jnp.arange(piece), S * Q)
        perm = (jnp.arange(width)[:, None] == src_rows[None, :]).astype(BF)
        piece_hot = (ids[:, None] == src_piece[None, :]).astype(F32)

        low = jax.nn.silu(cond.astype(F32)).astype(BF)
        biases = (bias_qv, b_proj, b_fc1, b_fc2, b_ada)
        sizes = [b.shape[0] for b in biases]
        small = jnp.concatenate(biases)
        packed = jnp.concatenate([small, low.reshape(-1)])[None]
        half = net.small_gather(packed)
        got = jnp.concatenate([half, net.core(half)], axis=0)
        nb = small.shape[0]
        bias_all = dotf(piece_hot, got[:, :nb].astype(F32), 1, 0)
        cuts = [sum(sizes[:i]) for i in range(len(sizes) + 1)]
        full_bias = [bias_all[:, cuts[i] : cuts[i + 1]].reshape(-1) for i in range(5)]
        low_rel = got.reshape(S, Q, -1)[:, 0, nb:].reshape(S * per, width)
        sh = net.shard_of(s, jnp.arange(S))
        lat_src = (sh[:, None] * per + jnp.arange(per)[None]).reshape(-1)
        cols = S // 2
        col = net.column_of(s, jnp.arange(cols))
        lat_dst = (col[:, None] * Q + (z + jnp.arange(Q)[None]) % Q).reshape(-1)
        lat_hot = (lat_dst[:, None] == lat_src[None, :]).astype(BF)
        mine = (jnp.arange(width)[:, None] == (me * piece + jnp.arange(piece))[None, :]).astype(BF)
        low_dst = dotf(lat_hot, low_rel, 1, 0).astype(BF)
        low_mine = dotf(low_dst, mine, 1, 0).astype(BF)
        cur = dotf(low_mine, w_ada, 1, 0).reshape(cols, Q, mods)
        for j in reversed(range(net.P)):
            h = cur.shape[0] // 2
            cur = cur[:h] + net.phase(cur[h:], j)
        cur = cur[0]
        part = net.small_rotate_sum([cur[r : r + 1] for r in range(Q)])
        mod = part + net.core(part) + full_bias[4][None]
        shift1, scale1, gate1, shift2, scale2, gate2 = jnp.split(mod, 6, axis=1)

        tok = collect(tokens)
        x = tok.astype(F32)
        wq = jnp.concatenate(net.gather(w_qkv), axis=0)
        wp = jnp.concatenate(net.gather(w_proj), axis=0)
        w1 = jnp.concatenate(net.gather(w_fc1), axis=0)
        dout = collect(d_out).astype(F32)
        blocks2 = net.gather(w_fc2)
        w2 = jnp.zeros((S, Q * fpiece, width), BF)
        sh_list = [net.shard_of(s, jnp.asarray(b)) for b in range(S)]
        def unroll(b):
            b = b.reshape(Q, fpiece, width)
            return jnp.roll(b, z, axis=0).reshape(Q * fpiece, width)

        for b in range(S):
            w2 = lax.dynamic_update_slice(w2, unroll(blocks2[b])[None], (sh_list[b], 0, 0))
        w2 = w2.reshape(hidden, width)

        n1, inv1 = norm_stats(x)
        a_in = (n1 * (1.0 + scale1) + shift1).astype(BF)
        a_rel = dotf(a_in, perm, 1, 0).astype(BF)
        bq = full_bias[0]
        bias_full = jnp.concatenate([bq[:width], jnp.zeros((width,), F32), bq[width:]])
        qkv_t = (dotf(wq, a_rel, 0, 1) + bias_full[:, None]).astype(BF)
        other_t = net.core(qkv_t[width:])
        mixed_t, lse = attention(qkv_t, other_t)
        mixed_rel = dotf(perm, mixed_t, 0, 0).astype(BF)
        attn_out = dotf(mixed_rel, wp, 0, 0) + full_bias[1][None]
        mid = x + gate1 * attn_out
        n2, inv2 = norm_stats(mid)
        m_in = (n2 * (1.0 + scale2) + shift2).astype(BF)
        m_rel = dotf(m_in, perm, 1, 0).astype(BF)
        up = dotf(m_rel, w1, 1, 0) + full_bias[2][None]
        act = gelu_tanh(up).astype(BF)
        ff = dotf(act, w2, 1, 0) + full_bias[3][None]
        output = give_back((mid + gate2 * ff).astype(BF))

        d_gate2 = jnp.sum(dout * ff, axis=0)
        d_ff = (gate2 * dout).astype(BF)
        db2 = jnp.sum(d_ff.astype(F32), axis=0)

        def w2_rows(b):
            start = sh_list[b] * (Q * fpiece)
            part = lax.dynamic_slice(act, (0, start), (act.shape[0], Q * fpiece))
            return dotf(part, d_ff, 0, 0)

        def seq_order(g):
            g = g.reshape(Q, fpiece, width)
            return jnp.roll(g, -z, axis=0).reshape(Q * fpiece, width)

        w2_other = jnp.concatenate([seq_order(w2_rows(b).astype(BF)) for b in range(S // 2, S)], axis=0)
        w2_own = jnp.concatenate([seq_order(w2_rows(b).astype(BF)) for b in range(S // 2)], axis=0)
        g_fc2 = net.reduce(w2_other, w2_own, fpiece)

        d_act = dotf(d_ff, w2, 1, 1)
        d_up = (gelu_slope(up) * d_act).astype(BF)
        db1 = jnp.sum(d_up.astype(F32), axis=0)
        hw = width // 2
        g_fc1 = net.reduce(dotf(m_rel[:, hw:], d_up, 0, 0), dotf(m_rel[:, :hw], d_up, 0, 0), piece)
        d_h2 = dotf(dotf(d_up, w1, 1, 1).astype(BF), perm, 1, 1)
        d_norm2, d_shift2, d_scale2 = norm_back(d_h2, n2, inv2, scale2)
        d_mid = dout + d_norm2
        d_gate1 = jnp.sum(d_mid * attn_out, axis=0)
        d_attn = (gate1 * d_mid).astype(BF)
        dbp = jnp.sum(d_attn.astype(F32), axis=0)
        g_proj = net.reduce(dotf(mixed_rel[hw:], d_attn, 1, 0), dotf(mixed_rel[:hw], d_attn, 1, 0), piece)
        d_mixed_rel = dotf(wp, d_attn, 1, 1).astype(BF)
        d_mixed_t = dotf(perm, d_mixed_rel, 1, 0).astype(BF)
        dq, dk0, dv0, dk1, dv1 = attention_back(qkv_t, other_t, d_mixed_t, lse)
        dkv1 = net.core(jnp.concatenate([dk1, dv1], axis=0)).astype(F32)
        dk = (dk0 + dkv1[:width]).astype(BF)
        dv = (dv0 + dkv1[width:]).astype(BF)
        d_qkv = jnp.concatenate([dq, dk, dv], axis=0)
        dbq = jnp.concatenate([jnp.sum(dq.astype(F32), axis=1), jnp.sum(dv.astype(F32), axis=1)])
        g_qkv = net.reduce(dotf(a_rel[:, hw:], d_qkv, 0, 1), dotf(a_rel[:, :hw], d_qkv, 0, 1), piece)
        d_h1 = dotf(dotf(d_qkv, wq, 0, 1).astype(BF), perm, 1, 1)
        d_norm1, d_shift1, d_scale1 = norm_back(d_h1, n1, inv1, scale1)
        grad_tokens = give_back((d_mid + d_norm1).astype(BF)).astype(F32)

        vec = jnp.concatenate(
            [dbq.reshape(S * Q, -1), dbp.reshape(S * Q, -1), db1.reshape(S * Q, -1), db2.reshape(S * Q, -1)],
            axis=1,
        )
        vec = lax.dot_general(
            piece_hot, vec, (((0,), (0,)), ((), ())), precision=HI, preferred_element_type=F32
        )
        h = vec.shape[0] // 2
        cur = vec[:h] + net.core(vec[h:])
        for j in reversed(range(net.P)):
            h = cur.shape[0] // 2
            cur = cur[:h] + net.phase(cur[h:], j)
        small_grad = net.small_rotate_sum([cur[r : r + 1] for r in range(Q)])[0]
        g_bq, g_bp, g_b1, g_b2 = (small_grad[cuts[i] : cuts[i + 1]] for i in range(4))

        d_mod = jnp.concatenate([d_shift1, d_scale1, d_gate1, d_shift2, d_scale2, d_gate2])[None]
        d_mod = (d_mod + net.core(d_mod)).astype(BF)
        d_mod = net.small_gather(d_mod)
        g_ada = dotf(low_mine, d_mod, 0, 0)
        nba = sizes[4]
        g_bada = lax.dynamic_slice(jnp.sum(d_mod.astype(F32), axis=0), (me * nba,), (nba,))
        d_low = dotf(d_mod, w_ada, 1, 1)
        lat_abs = (jnp.arange(latents)[:, None] == lat_dst[None, :]).astype(F32)
        d_low = lax.dot_general(
            lat_abs, d_low, (((1,), (0,)), ((), ())), precision=HI, preferred_element_type=F32
        )
        d_half = net.small_gather(d_low.reshape(1, -1))
        d_all = jnp.concatenate([d_half, net.core(d_half)], axis=0).reshape(S * Q, latents, piece)
        d_all = lax.dynamic_slice(d_all, (0, s * per, 0), (S * Q, per, piece))
        d_all = lax.dot_general(
            piece_hot,
            d_all.reshape(S * Q, per * piece),
            (((1,), (0,)), ((), ())),
            precision=HI,
            preferred_element_type=F32,
        )
        d_silu = d_all.reshape(S * Q, per, piece).transpose(1, 0, 2).reshape(per, width)
        grad_cond = jax.vjp(jax.nn.silu, cond.astype(F32))[1](d_silu)[0]
        return (
            output, grad_tokens, grad_cond, g_qkv, g_bq, g_proj, g_bp, g_fc1, g_b1, g_fc2, g_b2, g_ada, g_bada,
        )

    return body


def solution(mesh):
    tok = P("shard", "seq", None)
    mat = P(ALL, None)
    vec = P(ALL)
    weights = (mat, vec, mat, vec, mat, vec, mat, vec, mat, vec)
    return jax.shard_map(
        make_body(mesh.shape["shard"], mesh.shape["seq"]),
        mesh=mesh,
        in_specs=(tok, P("shard", None), tok) + weights,
        out_specs=(tok, tok, P("shard", None)) + weights,
        check_vma=False,
    )
```
